32 devices in a mesh: clus: 8 (over z, core), sub: 4 (over y, x).
Axes of the slice: x: 2, y: 2, z: 4, core: 2. Of those that a mesh axis runs over, the one named last changes fastest.
Arguments:
- right_side: float32 [8, 4, 896, 512], P('clus', 'sub'), may hold values from -6 to 6
- dual_operator: float32 [8, 4, 896, 896], P('clus', 'sub'), may hold values from -1 to 3
- corner_basis: float32 [8, 4, 24, 896], P('clus', 'sub'), may hold values from -0.1875 to 0.1875
- coarse_inverse: float32 [8, 96, 96], P('clus'), may hold values from -1 to 2
- corner_map: int32 [8, 96], P('clus'), may hold values from 0 to 95, each once within a row
- iface_counts: int32 [8, 4, 4], P('clus', 'sub'), may hold values from 0 to 16, as said below
Outputs:
- solution: float32 [8, 4, 896, 512], P('clus', 'sub')
- residual: float32 [8, 4, 896, 512], P('clus', 'sub')
The draws below stay inside these ranges and needn't reach their ends.
Inputs may be any that keep to these rules, and one draw needn't show every extreme that they name: `iface_counts`: symmetric in its last two dimensions with a zero diagonal; in every cluster one subdomain shares exactly 16 multipliers with every other subdomain of the cluster.
All inputs are finite; a program needn't handle non-finite values.
Results may differ from the reference program's by a relative error of at most 0.00011.
Values sent between devices are 32-bit elements; how exact they have to be, the bound alone decides.
A program may use at most 64 MiB of HBM per device.

```python
import math
import jax
import jax.numpy as jnp
from jax import lax

LOC = 896
NCOR = 24
XC = 128
CAP = 16
RHS = 512
ITERS = 3
CLUSTERS = 8
SUBS = 4
COARSE = 96


def draw_dual_operator(key, part):
    keys = jax.random.split(key, CLUSTERS * SUBS)

    def single(one_key):
        key_raw, key_diag, key_stiff = jax.random.split(one_key, 3)
        raw = jax.random.normal(key_raw, (LOC, LOC), jnp.float32)
        symmetric = (raw + raw.T) * (0.4 / math.sqrt(2.0 * LOC))
        diagonal = jax.random.uniform(key_diag, (LOC,), jnp.float32, 0.7, 1.3)
        stiffness = jnp.exp(jax.random.uniform(key_stiff, (), jnp.float32, math.log(0.5), math.log(2.0)))
        return (symmetric + jnp.diag(diagonal)) * stiffness
    return lax.map(single, keys).reshape(CLUSTERS, SUBS, LOC, LOC)


def draw_coarse_inverse(key, part):
    keys = jax.random.split(key, CLUSTERS)

    def single(one_key):
        raw = jax.random.normal(one_key, (COARSE, COARSE), jnp.float32)
        return jnp.eye(COARSE, dtype=jnp.float32) + raw * (0.8 / math.sqrt(COARSE))
    return lax.map(single, keys)


def draw_iface_counts(key, part):
    key_raw, key_star = jax.random.split(jax.random.fold_in(key, 7))
    raw = jax.random.randint(key_raw, (CLUSTERS, SUBS, SUBS), 0, CAP + 1)
    row_ids = jnp.arange(SUBS, dtype=jnp.int32)[:, None]
    col_ids = jnp.arange(SUBS, dtype=jnp.int32)[None, :]
    upper = jnp.where(col_ids > row_ids, raw, 0)
    symmetric = upper + jnp.swapaxes(upper, 1, 2)
    star = jax.random.randint(key_star, (CLUSTERS, 1, 1), 0, SUBS)
    touch = (row_ids[None] == star) | (col_ids[None] == star)
    result = jnp.where(touch, CAP, symmetric)
    result = jnp.where(row_ids[None] == col_ids[None], 0, result)
    return result.astype(jnp.int32)


def block_levels(key, dims, cuts, smallest, largest):
    def one(axis_at, shards_of):
        heights = jax.random.uniform(jax.random.fold_in(jax.random.fold_in(key, 6), axis_at), (shards_of,), jnp.float32, smallest / len(cuts), largest / len(cuts))
        return jnp.repeat(jnp.exp(heights), dims[axis_at] // shards_of).reshape((-1,) + (1,) * (len(dims) - axis_at - 1))

    level = one(*cuts[0])
    for cut in cuts[1:]:
        level = level * one(*cut)
    return level


def noise(stream_key, extent, scale, bound, cuts=(), kind=jnp.bfloat16):
    level = block_levels(stream_key, extent, cuts, -0.22, 0.18) if cuts else 1.0
    array = jax.random.normal(stream_key, extent, jnp.float32) * scale * level
    return jnp.minimum(jnp.maximum(array, -bound), bound).astype(kind)


def setup_inputs(seed: int = 0) -> dict:
    key_list = jax.random.split(jax.random.key(seed), 7)
    right_side = noise(key_list[0], (CLUSTERS, SUBS, LOC, RHS), 1.0, 6.0, ((0, 8), (1, 4)), jnp.float32)
    dual_operator = draw_dual_operator(jax.random.fold_in(key_list[6], 71), 0)
    corner_basis = noise(key_list[2], (CLUSTERS, SUBS, NCOR, LOC), LOC ** -0.5, 0.1875, ((0, 8), (1, 4)), jnp.float32)
    coarse_inverse = draw_coarse_inverse(jax.random.fold_in(key_list[6], 71), 0)
    corner_map = jax.vmap(lambda own: jax.random.permutation(own, COARSE))(jax.random.split(key_list[4], CLUSTERS)).reshape((CLUSTERS, COARSE)).astype(jnp.int32)
    iface_counts = draw_iface_counts(jax.random.fold_in(key_list[6], 71), 0)
    return {"right_side": right_side, "dual_operator": dual_operator, "corner_basis": corner_basis, "coarse_inverse": coarse_inverse, "corner_map": corner_map, "iface_counts": iface_counts}


spectrum_low = 0.5
spectrum_high = 3.0
center_value = (spectrum_high + spectrum_low) / 2.0
half_width = (spectrum_high - spectrum_low) / 2.0
sigma_one = center_value / half_width


def partner_rows(product, counts):
    finish = jnp.cumsum(counts, axis=2).astype(jnp.int32)
    starts = (finish - counts).astype(jnp.int32)
    position = (jnp.arange(LOC, dtype=jnp.int32) - 2 * XC)[None, None, :]
    source = jnp.sum((position[:, :, :, None] >= finish[:, :, None, :]).astype(jnp.int32), axis=3)
    usable = (position >= 0) & (source < SUBS)
    source = jnp.minimum(source, SUBS - 1).astype(jnp.int32)
    within = position - jnp.take_along_axis(starts, source, axis=2)
    theirs = jnp.take_along_axis(jnp.swapaxes(starts, 1, 2), source, axis=2)
    flat_index = jnp.where(usable, source * LOC + 2 * XC + theirs + within, 0).astype(jnp.int32)
    flat = product.reshape(CLUSTERS, SUBS * LOC, RHS)

    def pick(table, indices):
        return jnp.take(table, indices.reshape(-1), axis=0)

    inner = jax.vmap(pick)(flat, flat_index).reshape(CLUSTERS, SUBS, LOC, RHS)
    inner = jnp.where(usable[..., None], inner, jnp.zeros_like(inner))
    zeros = jnp.zeros((1, SUBS, XC, RHS), product.dtype)
    below = jnp.concatenate([zeros, product[:-1, :, XC:2 * XC]], axis=0)
    above = jnp.concatenate([product[1:, :, :XC], zeros], axis=0)
    return jnp.concatenate([below, above, inner[:, :, 2 * XC:]], axis=2)


def operator_apply(direction, dual_operator, corner_basis, coarse_inverse, corner_map, iface_counts):
    highest = lax.Precision.HIGHEST
    product = jnp.einsum('csij,csjr->csir', dual_operator, direction, precision=highest)
    assembled = product - partner_rows(product, iface_counts)
    corner_vals = jnp.einsum('csnl,cslr->csnr', corner_basis, direction, precision=highest)
    corner_vals = corner_vals.reshape(CLUSTERS, COARSE, RHS)

    def place(values, mapping):
        return jnp.zeros_like(values).at[mapping].set(values)

    coarse_rhs = jax.vmap(place)(corner_vals, corner_map)
    coarse_sol = jnp.einsum('cij,cjr->cir', coarse_inverse, coarse_rhs, precision=highest)
    back = jnp.take_along_axis(coarse_sol, corner_map[:, :, None].astype(jnp.int32), axis=1)
    back = back.reshape(CLUSTERS, SUBS, NCOR, RHS)
    return assembled + jnp.einsum('csnl,csnr->cslr', corner_basis, back, precision=highest)


def reference(right_side, dual_operator, corner_basis, coarse_inverse, corner_map, iface_counts):
    solution = jnp.zeros_like(right_side)
    residual = right_side
    ratio_now = 1.0 / sigma_one
    direction = right_side / center_value
    for iteration in range(ITERS):
        solution = solution + direction
        residual = residual - operator_apply(direction, dual_operator, corner_basis, coarse_inverse, corner_map, iface_counts)
        if iteration + 1 < ITERS:
            ratio_next = 1.0 / (2.0 * sigma_one - ratio_now)
            direction = (ratio_next * ratio_now) * direction + (2.0 * ratio_next / half_width) * residual
            ratio_now = ratio_next
    return solution, residual
```

```python
import functools

import jax
import jax.numpy as jnp
from jax import lax
from jax.experimental import pallas as pl
from jax.experimental.pallas import tpu as pltpu
from jax.sharding import PartitionSpec as P

XC = 128
CAP = 16
ITERS = 3
CHUNKS = 2
BLOCK = 320
VMEM_BYTES = 67043328

spectrum_low = 0.5
spectrum_high = 3.0
center_value = (spectrum_high + spectrum_low) / 2.0
half_width = (spectrum_high - spectrum_low) / 2.0
sigma_one = center_value / half_width

MESH = pl.DeviceIdType.MESH
F32 = jnp.float32
BF16 = jnp.bfloat16


def coefficients():
    ratio_now = 1.0 / sigma_one
    pairs = []
    for _ in range(ITERS - 1):
        ratio_next = 1.0 / (2.0 * sigma_one - ratio_now)
        pairs.append((ratio_next * ratio_now, 2.0 * ratio_next / half_width))
        ratio_now = ratio_next
    return pairs


def round_up(value, multiple):
    return -(-value // multiple) * multiple


def split(value):
    high = value.astype(BF16)
    return high, (value - high.astype(F32)).astype(BF16)


def kernel(
    nclus,
    nsub,
    rhs_hbm,
    op_hbm,
    basis_hbm,
    inv_hbm,
    map_hbm,
    counts_hbm,
    sol_ref,
    res_ref,
    op,
    basis_ref,
    inv_ref,
    map_ref,
    counts_ref,
    x_high,
    x_low,
    y_high,
    y_low,
    ahead,
    fixes,
    back_mat,
    basis_pad,
    sub_send,
    sub_recv,
    face_send,
    face_recv,
    load_sem,
    sub_send_sem,
    sub_recv_sem,
    face_send_sem,
    face_recv_sem,
):
    loc, ncols = rhs_hbm.shape
    ncor = basis_hbm.shape[0]
    coarse = inv_hbm.shape[0]
    per = CAP + ncor
    nsend = nsub * per
    width = ncols // CHUNKS
    edge = 2 * XC
    first = edge + round_up((nsub - 1) * CAP, 128)
    clus = lax.axis_index("clus")
    sub = lax.axis_index("sub")

    barrier = pltpu.get_barrier_semaphore()
    for offset in range(1, nsub):
        pl.semaphore_signal(
            barrier, inc=1, device_id=(clus, lax.rem(sub + offset, nsub)), device_id_type=MESH
        )

    @pl.when(clus > 0)
    def _():
        pl.semaphore_signal(barrier, inc=1, device_id=(clus - 1, sub), device_id_type=MESH)

    @pl.when(clus < nclus - 1)
    def _():
        pl.semaphore_signal(barrier, inc=1, device_id=(clus + 1, sub), device_id_type=MESH)

    small = [
        pltpu.make_async_copy(source, target, load_sem.at[2 + CHUNKS + i])
        for i, (source, target) in enumerate(
            (
                (map_hbm, map_ref),
                (inv_hbm, inv_ref),
                (counts_hbm, counts_ref),
                (basis_hbm, basis_ref),
            )
        )
    ]
    for copy in small:
        copy.start()
    spans = [slice(c * width, (c + 1) * width) for c in range(CHUNKS)]
    load_top = pltpu.make_async_copy(op_hbm.at[0:first], op.at[0:first], load_sem.at[0])
    load_low = pltpu.make_async_copy(op_hbm.at[first:loc], op.at[first:loc], load_sem.at[1])
    load_rhs = [
        pltpu.make_async_copy(rhs_hbm.at[:, span], res_ref.at[:, span], load_sem.at[2 + c])
        for c, span in enumerate(spans)
    ]
    load_rhs[0].start()
    load_top.start()
    for copy in load_rhs[1:]:
        copy.start()
    load_low.start()

    @pl.when(clus == 0)
    def _():
        face_recv[:, 0] = jnp.zeros(face_recv.shape[:1] + face_recv.shape[2:], F32)

    @pl.when(clus == nclus - 1)
    def _():
        face_recv[:, 1] = jnp.zeros(face_recv.shape[:1] + face_recv.shape[2:], F32)

    basis_pad[...] = jnp.zeros_like(basis_pad)
    for copy in small:
        copy.wait()
    onehot = jnp.where(
        lax.broadcasted_iota(jnp.int32, (coarse, coarse), 0) == map_ref[...], 1.0, 0.0
    ).astype(BF16)
    chosen_columns = [
        jnp.dot(part, onehot, preferred_element_type=F32).astype(BF16)
        for part in split(inv_ref[...])
    ]
    t_high, t_low = [
        lax.dot_general(
            onehot, part, (((0,), (0,)), ((), ())), preferred_element_type=F32
        ).astype(BF16)
        for part in chosen_columns
    ]
    basis = basis_ref[...]
    basis_pad[pl.ds(pl.multiple_of(sub * ncor, 8), ncor), :] = basis
    p_high, p_low = split(basis_pad[...])
    corner_rows = (
        jnp.dot(t_high, p_high, preferred_element_type=F32)
        + jnp.dot(t_high, p_low, preferred_element_type=F32)
        + jnp.dot(t_low, p_high, preferred_element_type=F32)
    )

    nface = nsub * CAP
    reach = first - edge
    slot_row = lax.broadcasted_iota(jnp.int32, (nface, reach), 0)
    place = lax.broadcasted_iota(jnp.int32, (nface, reach), 1)
    inside = slot_row % CAP
    owner = slot_row // CAP
    begin = jnp.int32(0)
    picked = jnp.zeros((nface, reach), F32)
    for p in range(nsub):
        count = counts_ref[0, p]
        hit = (owner == p) & (inside < count) & (place == inside + begin)
        picked = jnp.where(hit, 1.0, picked)
        begin = begin + count
    pad = back_mat.shape[1] - 3 * ncor - 2 * nface

    def build_back():
        b_high, b_low = split(basis)
        spread = jnp.concatenate(
            [
                jnp.zeros((nface, edge), F32),
                -picked,
                jnp.zeros((nface, loc - first), F32),
            ],
            axis=1,
        )
        stacked = [b_high.astype(F32), b_high.astype(F32), b_low.astype(F32), spread, spread]
        if pad:
            stacked.append(jnp.zeros((pad, loc), F32))
        back_mat[...] = jnp.transpose(jnp.concatenate(stacked, axis=0)).astype(BF16)

    def put_split(begin_row, high, low):
        rows = high.shape[0]
        x_high[begin_row : begin_row + rows, :] = high
        x_low[begin_row : begin_row + rows, :] = low

    def put_rows(begin_row, value):
        put_split(begin_row, *split(value))

    def put_direction(columns, value, begin_row, end_row):
        high, low = split(value)
        y_high[begin_row:end_row, columns] = high
        y_low[begin_row:end_row, columns] = low

    def times(begin_row, end_row, columns):
        high = x_high[begin_row:end_row, :]
        rows = jnp.concatenate([high, high, x_low[begin_row:end_row, :]], axis=1)
        top = y_high[:, columns]
        deep = jnp.concatenate([top, y_low[:, columns], top], axis=0)
        return jnp.dot(rows, deep, preferred_element_type=F32)

    def begin_part(c):
        load_rhs[c].wait()
        put_direction(spans[c], res_ref[:, spans[c]] * (1.0 / center_value), 0, loc)

    put_rows(nface, corner_rows)
    begin_part(0)
    load_top.wait()
    put_rows(nsend, op[0:edge])
    chosen = picked.astype(BF16)
    m_high, m_low = split(op[edge:first])
    put_split(
        0,
        jnp.dot(chosen, m_high, preferred_element_type=F32).astype(BF16),
        jnp.dot(chosen, m_low, preferred_element_type=F32).astype(BF16),
    )

    for c in range(1, CHUNKS):
        begin_part(c)

    near = jnp.where(clus > 0, 1, 0) + jnp.where(clus < nclus - 1, 1, 0)
    pl.semaphore_wait(barrier, nsub - 1 + near)

    def sub_copy(slot, offset):
        partner = lax.rem(sub + offset, nsub)
        return pltpu.make_async_remote_copy(
            src_ref=sub_send.at[slot, partner],
            dst_ref=sub_recv.at[slot, sub],
            send_sem=sub_send_sem.at[slot, offset - 1],
            recv_sem=sub_recv_sem.at[slot, offset - 1],
            device_id=(clus, partner),
            device_id_type=MESH,
        )

    def face_copy(slot, side):
        return pltpu.make_async_remote_copy(
            src_ref=face_send.at[slot, side],
            dst_ref=face_recv.at[slot, side],
            send_sem=face_send_sem.at[slot, side],
            recv_sem=face_recv_sem.at[slot, side],
            device_id=(clus + (1 if side == 0 else -1), sub),
            device_id_type=MESH,
        )

    def send_part(iteration, c):
        columns = spans[c]
        slot = iteration * CHUNKS + c
        middle = (nsend + edge) // 2
        lead = jnp.concatenate([times(0, middle, columns), times(middle, nsend + edge, columns)], axis=0)
        for p in range(nsub):
            sub_send[slot, p, 0:CAP] = lead[p * CAP : (p + 1) * CAP]
            sub_send[slot, p, CAP:per] = lead[nface + p * ncor : nface + (p + 1) * ncor]
        face_send[slot, 0] = lead[nsend + XC : nsend + edge]
        face_send[slot, 1] = lead[nsend : nsend + XC]
        for offset in range(1, nsub):
            sub_copy(slot, offset).start()

        @pl.when(clus < nclus - 1)
        def _():
            face_copy(slot, 0).start()

        @pl.when(clus > 0)
        def _():
            face_copy(slot, 1).start()

    def advance(iteration, c, begin_row, end_row, product):
        rows = slice(begin_row, end_row)
        columns = spans[c]
        value = res_ref[rows, columns]
        if iteration == 0:
            moved = value * (1.0 / center_value)
            sol_ref[rows, columns] = moved
        else:
            fix = fixes[rows, columns]
            value = value - fix
            moved = ahead[rows, columns] - coefficients()[iteration - 1][1] * fix
            sol_ref[rows, columns] = sol_ref[rows, columns] + moved
        value = value - product
        res_ref[rows, columns] = value
        if iteration + 1 < ITERS:
            keep, gain = coefficients()[iteration]
            ahead[rows, columns] = keep * moved + gain * value

    def rest_part(iteration):
        tail = times(nsend + edge, nsend + loc, slice(0, ncols))
        for c in range(CHUNKS):
            slot = iteration * CHUNKS + c
            sub_recv[slot, pl.ds(sub, 1)] = sub_send[slot, pl.ds(sub, 1)]
            advance(iteration, c, 0, XC, face_send[slot, 1])
            advance(iteration, c, XC, edge, face_send[slot, 0])
        for c in range(CHUNKS):
            advance(iteration, c, edge, loc, tail[:, spans[c]])

    def receive_part(iteration, c):
        columns = spans[c]
        slot = iteration * CHUNKS + c
        for offset in range(1, nsub):
            sub_copy(slot, offset).wait_recv()

        @pl.when(clus > 0)
        def _():
            face_copy(slot, 0).wait_recv()

        @pl.when(clus < nclus - 1)
        def _():
            face_copy(slot, 1).wait_recv()

        back = sub_recv[slot, 0, CAP:per]
        for p in range(1, nsub):
            back = back + sub_recv[slot, p, CAP:per]
        faces = jnp.concatenate([sub_recv[slot, p, 0:CAP] for p in range(nsub)], axis=0)
        k_high, k_low = [part.astype(F32) for part in split(back)]
        f_high, f_low = [part.astype(F32) for part in split(faces)]
        gathered = [k_high, k_low, k_high, f_high, f_low]
        if pad:
            gathered.append(jnp.zeros((pad, width), F32))
        operand = jnp.concatenate(gathered, axis=0).astype(BF16)
        across = face_recv[slot].reshape(edge, width)
        bounds = [0, edge] + list(range(edge + BLOCK, loc, BLOCK)) + [loc]
        for low, high in zip(bounds[:-1], bounds[1:]):
            fix = jnp.dot(back_mat[low:high, :], operand, preferred_element_type=F32)
            if low == 0:
                fix = fix - across
            if iteration + 1 < ITERS:
                fixes[low:high, columns] = fix
                moved = ahead[low:high, columns] - coefficients()[iteration][1] * fix
                put_direction(columns, moved, low, high)
            else:
                res_ref[low:high, columns] = res_ref[low:high, columns] - fix

    for iteration in range(ITERS):
        for c in range(CHUNKS):
            if iteration:
                receive_part(iteration - 1, c)
            send_part(iteration, c)
        if iteration == 0:
            load_low.wait()
            put_rows(nsend + edge, op[edge:loc])
            build_back()
        rest_part(iteration)
    for c in range(CHUNKS):
        receive_part(ITERS - 1, c)

    for slot in range(ITERS * CHUNKS):
        for offset in range(1, nsub):
            sub_copy(slot, offset).wait_send()

        @pl.when(clus < nclus - 1)
        def _():
            face_copy(slot, 0).wait_send()

        @pl.when(clus > 0)
        def _():
            face_copy(slot, 1).wait_send()


def flush(sol_vmem, res_vmem, sol_hbm, res_hbm, sem):
    first = pltpu.make_async_copy(sol_vmem, sol_hbm, sem.at[0])
    second = pltpu.make_async_copy(res_vmem, res_hbm, sem.at[1])
    first.start()
    second.start()
    first.wait()
    second.wait()


def on_device(right_side, dual_operator, corner_basis, coarse_inverse, corner_map, iface_counts):
    nsub = lax.axis_size("sub")
    nclus = lax.axis_size("clus")
    loc, ncols = right_side.shape[2:]
    ncor = corner_basis.shape[2]
    per = CAP + ncor
    slots = ITERS * CHUNKS
    width = ncols // CHUNKS
    rows = nsub * per + loc
    depth = round_up(3 * ncor + 2 * nsub * CAP, 128)
    vmem = pl.BlockSpec(memory_space=pltpu.VMEM)
    hbm = pl.BlockSpec(memory_space=pltpu.HBM)
    shape = jax.ShapeDtypeStruct((loc, ncols), F32)
    dma = pltpu.SemaphoreType.DMA
    outs = pl.pallas_call(
        functools.partial(kernel, nclus, nsub),
        out_shape=(pltpu.VMEM(shape.shape, F32), pltpu.VMEM(shape.shape, F32)),
        in_specs=[hbm] * 6,
        out_specs=(vmem, vmem),
        scratch_shapes=[
            pltpu.VMEM((loc, loc), F32),
            pltpu.VMEM((ncor, loc), F32),
            pltpu.VMEM(coarse_inverse.shape[1:], F32),
            pltpu.VMEM(corner_map.shape, jnp.int32),
            pltpu.SMEM(iface_counts.shape[1:], jnp.int32),
            pltpu.VMEM((rows, loc), BF16),
            pltpu.VMEM((rows, loc), BF16),
            pltpu.VMEM((loc, ncols), BF16),
            pltpu.VMEM((loc, ncols), BF16),
            pltpu.VMEM((loc, ncols), F32),
            pltpu.VMEM((loc, ncols), F32),
            pltpu.VMEM((loc, depth), BF16),
            pltpu.VMEM((nsub * ncor, loc), F32),
            pltpu.VMEM((slots, nsub, per, width), F32),
            pltpu.VMEM((slots, nsub, per, width), F32),
            pltpu.VMEM((slots, 2, XC, width), F32),
            pltpu.VMEM((slots, 2, XC, width), F32),
            dma((6 + CHUNKS,)),
            dma((slots, nsub - 1)),
            dma((slots, nsub - 1)),
            dma((slots, 2)),
            dma((slots, 2)),
        ],
        compiler_params=pltpu.CompilerParams(
            collective_id=0, has_side_effects=True, vmem_limit_bytes=VMEM_BYTES - 2 * loc * ncols * 4 - 32 * 1024
        ),
    )(
        right_side[0, 0],
        dual_operator[0, 0],
        corner_basis[0, 0],
        coarse_inverse[0],
        corner_map,
        iface_counts[0],
    )
    outs = pl.pallas_call(
        flush,
        out_shape=(shape, shape),
        in_specs=[pl.BlockSpec(memory_space=pl.ANY)] * 2,
        out_specs=(hbm, hbm),
        scratch_shapes=[dma((2,))],
        compiler_params=pltpu.CompilerParams(vmem_limit_bytes=4 * 1024 * 1024),
    )(*outs)
    return outs[0][None, None], outs[1][None, None]


def solution(mesh):
    placed = (
        P("clus", "sub", None, None),
        P("clus", "sub", None, None),
        P("clus", "sub", None, None),
        P("clus", None, None),
        P("clus", None),
        P("clus", "sub", None),
    )
    return jax.shard_map(
        on_device,
        mesh=mesh,
        in_specs=placed,
        out_specs=(P("clus", "sub", None, None), P("clus", "sub", None, None)),
        check_vma=False,
    )
```

```python
import functools

import jax
import jax.numpy as jnp
from jax import lax
from jax.experimental import pallas as pl
from jax.experimental.pallas import tpu as pltpu
from jax.sharding import PartitionSpec as P

XC = 128
CAP = 16
ITERS = 3
CHUNKS = 2
BLOCK = 320
VMEM_BYTES = 67043328

spectrum_low = 0.5
spectrum_high = 3.0
center_value = (spectrum_high + spectrum_low) / 2.0
half_width = (spectrum_high - spectrum_low) / 2.0
sigma_one = center_value / half_width

MESH = pl.DeviceIdType.MESH
F32 = jnp.float32
BF16 = jnp.bfloat16


def coefficients():
    ratio_now = 1.0 / sigma_one
    pairs = []
    for _ in range(ITERS - 1):
        ratio_next = 1.0 / (2.0 * sigma_one - ratio_now)
        pairs.append((ratio_next * ratio_now, 2.0 * ratio_next / half_width))
        ratio_now = ratio_next
    return pairs


def round_up(value, multiple):
    return -(-value // multiple) * multiple


def split(value):
    high = value.astype(BF16)
    return high, (value - high.astype(F32)).astype(BF16)


def kernel(
    nclus,
    nsub,
    rhs_hbm,
    op_hbm,
    basis_hbm,
    inv_hbm,
    map_hbm,
    counts_hbm,
    sol_ref,
    res_ref,
    op,
    basis_ref,
    inv_ref,
    map_ref,
    counts_ref,
    x_high,
    x_low,
    y_high,
    y_low,
    ahead,
    fixes,
    back_mat,
    basis_pad,
    sub_send,
    sub_recv,
    face_send,
    face_recv,
    load_sem,
    sub_send_sem,
    sub_recv_sem,
    face_send_sem,
    face_recv_sem,
):
    loc, ncols = rhs_hbm.shape
    ncor = basis_hbm.shape[0]
    coarse = inv_hbm.shape[0]
    per = CAP + ncor
    nsend = nsub * per
    width = ncols // CHUNKS
    edge = 2 * XC
    first = edge + round_up((nsub - 1) * CAP, 128)
    clus = lax.axis_index("clus")
    sub = lax.axis_index("sub")

    barrier = pltpu.get_barrier_semaphore()
    for offset in range(1, nsub):
        pl.semaphore_signal(
            barrier, inc=1, device_id=(clus, lax.rem(sub + offset, nsub)), device_id_type=MESH
        )

    @pl.when(clus > 0)
    def _():
        pl.semaphore_signal(barrier, inc=1, device_id=(clus - 1, sub), device_id_type=MESH)

    @pl.when(clus < nclus - 1)
    def _():
        pl.semaphore_signal(barrier, inc=1, device_id=(clus + 1, sub), device_id_type=MESH)

    small = [
        pltpu.make_async_copy(source, target, load_sem.at[2 + CHUNKS + i])
        for i, (source, target) in enumerate(
            (
                (map_hbm, map_ref),
                (inv_hbm, inv_ref),
                (counts_hbm, counts_ref),
                (basis_hbm, basis_ref),
            )
        )
    ]
    for copy in small:
        copy.start()
    spans = [slice(c * width, (c + 1) * width) for c in range(CHUNKS)]
    load_top = pltpu.make_async_copy(op_hbm.at[0:first], op.at[0:first], load_sem.at[0])
    load_low = pltpu.make_async_copy(op_hbm.at[first:loc], op.at[first:loc], load_sem.at[1])
    load_rhs = [
        pltpu.make_async_copy(rhs_hbm.at[:, span], res_ref.at[:, span], load_sem.at[2 + c])
        for c, span in enumerate(spans)
    ]
    load_rhs[0].start()
    load_top.start()
    for copy in load_rhs[1:]:
        copy.start()
    load_low.start()

    @pl.when(clus == 0)
    def _():
        face_recv[:, 0] = jnp.zeros(face_recv.shape[:1] + face_recv.shape[2:], F32)

    @pl.when(clus == nclus - 1)
    def _():
        face_recv[:, 1] = jnp.zeros(face_recv.shape[:1] + face_recv.shape[2:], F32)

    basis_pad[...] = jnp.zeros_like(basis_pad)
    for copy in small:
        copy.wait()
    onehot = jnp.where(
        lax.broadcasted_iota(jnp.int32, (coarse, coarse), 0) == map_ref[...], 1.0, 0.0
    ).astype(BF16)
    chosen_columns = [
        jnp.dot(part, onehot, preferred_element_type=F32).astype(BF16)
        for part in split(inv_ref[...])
    ]
    t_high, t_low = [
        lax.dot_general(
            onehot, part, (((0,), (0,)), ((), ())), preferred_element_type=F32
        ).astype(BF16)
        for part in chosen_columns
    ]
    basis = basis_ref[...]
    basis_pad[pl.ds(pl.multiple_of(sub * ncor, 8), ncor), :] = basis
    p_high, p_low = split(basis_pad[...])
    corner_rows = (
        jnp.dot(t_high, p_high, preferred_element_type=F32)
        + jnp.dot(t_high, p_low, preferred_element_type=F32)
        + jnp.dot(t_low, p_high, preferred_element_type=F32)
    )

    nface = nsub * CAP
    reach = first - edge
    slot_row = lax.broadcasted_iota(jnp.int32, (nface, reach), 0)
    place = lax.broadcasted_iota(jnp.int32, (nface, reach), 1)
    inside = slot_row % CAP
    owner = slot_row // CAP
    begin = jnp.int32(0)
    picked = jnp.zeros((nface, reach), F32)
    for p in range(nsub):
        count = counts_ref[0, p]
        hit = (owner == p) & (inside < count) & (place == inside + begin)
        picked = jnp.where(hit, 1.0, picked)
        begin = begin + count
    pad = back_mat.shape[1] - 3 * ncor - 2 * nface

    def build_back():
        b_high, b_low = split(basis)
        spread = jnp.concatenate(
            [
                jnp.zeros((nface, edge), F32),
                -picked,
                jnp.zeros((nface, loc - first), F32),
            ],
            axis=1,
        )
        stacked = [b_high.astype(F32), b_high.astype(F32), b_low.astype(F32), spread, spread]
        if pad:
            stacked.append(jnp.zeros((pad, loc), F32))
        back_mat[...] = jnp.transpose(jnp.concatenate(stacked, axis=0)).astype(BF16)

    def put_split(begin_row, high, low):
        rows = high.shape[0]
        x_high[begin_row : begin_row + rows, :] = high
        x_low[begin_row : begin_row + rows, :] = low

    def put_rows(begin_row, value):
        put_split(begin_row, *split(value))

    def put_direction(columns, value, begin_row, end_row):
        high, low = split(value)
        y_high[begin_row:end_row, columns] = high
        y_low[begin_row:end_row, columns] = low

    def times(begin_row, end_row, columns):
        high = x_high[begin_row:end_row, :]
        rows = jnp.concatenate([high, high, x_low[begin_row:end_row, :]], axis=1)
        top = y_high[:, columns]
        deep = jnp.concatenate([top, y_low[:, columns], top], axis=0)
        return jnp.dot(rows, deep, preferred_element_type=F32)

    def begin_part(c):
        load_rhs[c].wait()
        put_direction(spans[c], res_ref[:, spans[c]] * (1.0 / center_value), 0, loc)

    put_rows(nface, corner_rows)
    begin_part(0)
    load_top.wait()
    put_rows(nsend, op[0:edge])
    chosen = picked.astype(BF16)
    m_high, m_low = split(op[edge:first])
    put_split(
        0,
        jnp.dot(chosen, m_high, preferred_element_type=F32).astype(BF16),
        jnp.dot(chosen, m_low, preferred_element_type=F32).astype(BF16),
    )

    near = jnp.where(clus > 0, 1, 0) + jnp.where(clus < nclus - 1, 1, 0)
    pl.semaphore_wait(barrier, nsub - 1 + near)

    def sub_copy(slot, offset):
        partner = lax.rem(sub + offset, nsub)
        return pltpu.make_async_remote_copy(
            src_ref=sub_send.at[slot, partner],
            dst_ref=sub_recv.at[slot, sub],
            send_sem=sub_send_sem.at[slot, offset - 1],
            recv_sem=sub_recv_sem.at[slot, offset - 1],
            device_id=(clus, partner),
            device_id_type=MESH,
        )

    def face_copy(slot, side):
        return pltpu.make_async_remote_copy(
            src_ref=face_send.at[slot, side],
            dst_ref=face_recv.at[slot, side],
            send_sem=face_send_sem.at[slot, side],
            recv_sem=face_recv_sem.at[slot, side],
            device_id=(clus + (1 if side == 0 else -1), sub),
            device_id_type=MESH,
        )

    def send_part(iteration, c):
        columns = spans[c]
        slot = iteration * CHUNKS + c
        middle = (nsend + edge) // 2
        lead = jnp.concatenate([times(0, middle, columns), times(middle, nsend + edge, columns)], axis=0)
        for p in range(nsub):
            sub_send[slot, p, 0:CAP] = lead[p * CAP : (p + 1) * CAP]
            sub_send[slot, p, CAP:per] = lead[nface + p * ncor : nface + (p + 1) * ncor]
        face_send[slot, 0] = lead[nsend + XC : nsend + edge]
        face_send[slot, 1] = lead[nsend : nsend + XC]
        for offset in range(1, nsub):
            sub_copy(slot, offset).start()

        @pl.when(clus < nclus - 1)
        def _():
            face_copy(slot, 0).start()

        @pl.when(clus > 0)
        def _():
            face_copy(slot, 1).start()

    def advance(iteration, c, begin_row, end_row, product):
        rows = slice(begin_row, end_row)
        columns = spans[c]
        value = res_ref[rows, columns]
        if iteration == 0:
            moved = value * (1.0 / center_value)
            sol_ref[rows, columns] = moved
        else:
            fix = fixes[rows, columns]
            value = value - fix
            moved = ahead[rows, columns] - coefficients()[iteration - 1][1] * fix
            sol_ref[rows, columns] = sol_ref[rows, columns] + moved
        value = value - product
        res_ref[rows, columns] = value
        if iteration + 1 < ITERS:
            keep, gain = coefficients()[iteration]
            ahead[rows, columns] = keep * moved + gain * value

    def rest_part(iteration):
        tail = times(nsend + edge, nsend + loc, slice(0, ncols))
        for c in range(CHUNKS):
            slot = iteration * CHUNKS + c
            sub_recv[slot, pl.ds(sub, 1)] = sub_send[slot, pl.ds(sub, 1)]
            advance(iteration, c, 0, XC, face_send[slot, 1])
            advance(iteration, c, XC, edge, face_send[slot, 0])
        for c in range(CHUNKS):
            advance(iteration, c, edge, loc, tail[:, spans[c]])

    def receive_part(iteration, c):
        columns = spans[c]
        slot = iteration * CHUNKS + c
        for offset in range(1, nsub):
            sub_copy(slot, offset).wait_recv()

        @pl.when(clus > 0)
        def _():
            face_copy(slot, 0).wait_recv()

        @pl.when(clus < nclus - 1)
        def _():
            face_copy(slot, 1).wait_recv()

        back = sub_recv[slot, 0, CAP:per]
        for p in range(1, nsub):
            back = back + sub_recv[slot, p, CAP:per]
        faces = jnp.concatenate([sub_recv[slot, p, 0:CAP] for p in range(nsub)], axis=0)
        k_high, k_low = [part.astype(F32) for part in split(back)]
        f_high, f_low = [part.astype(F32) for part in split(faces)]
        gathered = [k_high, k_low, k_high, f_high, f_low]
        if pad:
            gathered.append(jnp.zeros((pad, width), F32))
        operand = jnp.concatenate(gathered, axis=0).astype(BF16)
        across = face_recv[slot].reshape(edge, width)
        bounds = [0, edge] + list(range(edge + BLOCK, loc, BLOCK)) + [loc]
        for low, high in zip(bounds[:-1], bounds[1:]):
            fix = jnp.dot(back_mat[low:high, :], operand, preferred_element_type=F32)
            if low == 0:
                fix = fix - across
            if iteration + 1 < ITERS:
                fixes[low:high, columns] = fix
                moved = ahead[low:high, columns] - coefficients()[iteration][1] * fix
                put_direction(columns, moved, low, high)
            else:
                res_ref[low:high, columns] = res_ref[low:high, columns] - fix

    for iteration in range(ITERS):
        for c in range(CHUNKS):
            if iteration:
                receive_part(iteration - 1, c)
            elif c:
                begin_part(c)
            send_part(iteration, c)
        if iteration == 0:
            load_low.wait()
            put_rows(nsend + edge, op[edge:loc])
            build_back()
        rest_part(iteration)
    for c in range(CHUNKS):
        receive_part(ITERS - 1, c)

    for slot in range(ITERS * CHUNKS):
        for offset in range(1, nsub):
            sub_copy(slot, offset).wait_send()

        @pl.when(clus < nclus - 1)
        def _():
            face_copy(slot, 0).wait_send()

        @pl.when(clus > 0)
        def _():
            face_copy(slot, 1).wait_send()


def flush(sol_vmem, res_vmem, sol_hbm, res_hbm, sem):
    first = pltpu.make_async_copy(sol_vmem, sol_hbm, sem.at[0])
    second = pltpu.make_async_copy(res_vmem, res_hbm, sem.at[1])
    first.start()
    second.start()
    first.wait()
    second.wait()


def on_device(right_side, dual_operator, corner_basis, coarse_inverse, corner_map, iface_counts):
    nsub = lax.axis_size("sub")
    nclus = lax.axis_size("clus")
    loc, ncols = right_side.shape[2:]
    ncor = corner_basis.shape[2]
    per = CAP + ncor
    slots = ITERS * CHUNKS
    width = ncols // CHUNKS
    rows = nsub * per + loc
    depth = round_up(3 * ncor + 2 * nsub * CAP, 128)
    vmem = pl.BlockSpec(memory_space=pltpu.VMEM)
    hbm = pl.BlockSpec(memory_space=pltpu.HBM)
    shape = jax.ShapeDtypeStruct((loc, ncols), F32)
    dma = pltpu.SemaphoreType.DMA
    outs = pl.pallas_call(
        functools.partial(kernel, nclus, nsub),
        out_shape=(pltpu.VMEM(shape.shape, F32), pltpu.VMEM(shape.shape, F32)),
        in_specs=[hbm] * 6,
        out_specs=(vmem, vmem),
        scratch_shapes=[
            pltpu.VMEM((loc, loc), F32),
            pltpu.VMEM((ncor, loc), F32),
            pltpu.VMEM(coarse_inverse.shape[1:], F32),
            pltpu.VMEM(corner_map.shape, jnp.int32),
            pltpu.SMEM(iface_counts.shape[1:], jnp.int32),
            pltpu.VMEM((rows, loc), BF16),
            pltpu.VMEM((rows, loc), BF16),
            pltpu.VMEM((loc, ncols), BF16),
            pltpu.VMEM((loc, ncols), BF16),
            pltpu.VMEM((loc, ncols), F32),
            pltpu.VMEM((loc, ncols), F32),
            pltpu.VMEM((loc, depth), BF16),
            pltpu.VMEM((nsub * ncor, loc), F32),
            pltpu.VMEM((slots, nsub, per, width), F32),
            pltpu.VMEM((slots, nsub, per, width), F32),
            pltpu.VMEM((slots, 2, XC, width), F32),
            pltpu.VMEM((slots, 2, XC, width), F32),
            dma((6 + CHUNKS,)),
            dma((slots, nsub - 1)),
            dma((slots, nsub - 1)),
            dma((slots, 2)),
            dma((slots, 2)),
        ],
        compiler_params=pltpu.CompilerParams(
            collective_id=0, has_side_effects=True, vmem_limit_bytes=VMEM_BYTES - 2 * loc * ncols * 4 - 32 * 1024
        ),
    )(
        right_side[0, 0],
        dual_operator[0, 0],
        corner_basis[0, 0],
        coarse_inverse[0],
        corner_map,
        iface_counts[0],
    )
    outs = pl.pallas_call(
        flush,
        out_shape=(shape, shape),
        in_specs=[pl.BlockSpec(memory_space=pl.ANY)] * 2,
        out_specs=(hbm, hbm),
        scratch_shapes=[dma((2,))],
        compiler_params=pltpu.CompilerParams(vmem_limit_bytes=4 * 1024 * 1024),
    )(*outs)
    return outs[0][None, None], outs[1][None, None]


def solution(mesh):
    placed = (
        P("clus", "sub", None, None),
        P("clus", "sub", None, None),
        P("clus", "sub", None, None),
        P("clus", None, None),
        P("clus", None),
        P("clus", "sub", None),
    )
    return jax.shard_map(
        on_device,
        mesh=mesh,
        in_specs=placed,
        out_specs=(P("clus", "sub", None, None), P("clus", "sub", None, None)),
        check_vma=False,
    )
```
